256 devices in a mesh: dp: 2 (over core), ctx: 16 (over z_hi, y), exp: 8 (over x, z_lo).
Axes of the slice: x: 4, y: 4, z: 8 (z_hi: 4, z_lo: 2; z = z_hi * 2 + z_lo), core: 2. Of those that a mesh axis runs over, the one named last changes fastest.
Arguments:
- tokens: bfloat16 [2, 2048, 2560], P('dp', 'ctx'), may hold values from -6 to 6
- queries: bfloat16 [2, 2048, 16, 576], P('dp', 'ctx', 'exp'), may hold values from -240 to 240
- kv_weight: bfloat16 [2560, 576], P('exp'), may hold values from -0.125 to 0.125
- kv_gain: bfloat16 [512], replicated, may hold values from 0.5 to 1.5
- uv_weight: bfloat16 [16, 512, 128], P('exp'), may hold values from -0.75 to 0.75
- out_weight: bfloat16 [2048, 2560], P('exp'), may hold values from -0.5 to 0.5
- post_gain: bfloat16 [2560], replicated, may hold values from 0.5 to 1.5
- router_weight: bfloat16 [2560, 32], replicated, may hold values from -0.125 to 0.125
- expert_ids: int32 [2, 2048, 6], P('dp', 'ctx'), may hold values from 0 to 31, all different within a row; in each aligned block of 128 rows (0 to 127, 128 to 255, ..., all dimensions but the last counted through in order) at most 32 rows name the same one
- doc_ids: int32 [2, 2048], P('dp', 'ctx'), may hold values from 0 to 3, never falling along the last dimension, each value on 1 to 1024 neighbouring positions
- gate_weight: bfloat16 [32, 2560, 1536], P('ctx', None, 'exp'), may hold values from -0.125 to 0.125
- up_weight: bfloat16 [32, 2560, 1536], P('ctx', None, 'exp'), may hold values from -0.125 to 0.125
- down_weight: bfloat16 [32, 1536, 2560], P('ctx', 'exp'), may hold values from -0.15625 to 0.15625
- cotangent: bfloat16 [2, 2048, 2560], P('dp', 'ctx'), may hold values from -6 to 6
Outputs:
- layer_out: bfloat16 [2, 2048, 2560], P('dp', 'ctx')
- router_grad: float32 [2560, 32], replicated
- gate_grad: bfloat16 [32, 2560, 1536], P('ctx', 'dp', 'exp')
- up_grad: bfloat16 [32, 2560, 1536], P('ctx', 'dp', 'exp')
- down_grad: bfloat16 [32, 1536, 2560], P('ctx', 'exp', 'dp')
The draws below stay inside these ranges and needn't reach their ends.
Inputs may be any that keep to these rules, and one draw needn't show every extreme that they name: `expert_ids`: in each aligned block of 128 positions of a sequence no expert is named by more than 32 of the block's assignments; the experts of one token differ. `doc_ids`: document numbers never fall along a sequence; a document has at most 1024 positions.
All inputs are finite; a program needn't handle non-finite values.
Results may differ from the reference program's by a relative error of at most 0.023.
The reference program's roundings to bfloat16 on the way count: a program that leaves them out, or rounds other values in their place, can miss the bound.
Values may be sent and summed in bfloat16 or wider, within the bound.
No kernel may reach another device: no remote copies, remote signals or barrier semaphores. Data moves between devices by JAX's collectives and lax.ppermute only.
A program may use at most 128 MiB of HBM per device.

```python
import math
import jax
import jax.numpy as jnp
import numpy as np
from jax import lax

D = 2560
HEADS = 16
LAT = 512
ROPE = 64
NOPE = 128
VH = 128
FFE = 1536
TOPK = 6
DOCS = 4
SEQ_DEV = 128
BATCH = 2
SEQ = 2048
EXPERTS = 32
CAP = 32
N_CTX = 16
N_EXP = 8


def draw_queries(key, part):
    first_key = jax.random.fold_in(jax.random.fold_in(key, 11), 0)
    shape = (BATCH, SEQ, HEADS, LAT + ROPE)
    base = jnp.clip(jax.random.normal(first_key, shape, jnp.float32), -6.0, 6.0)
    return base.astype(jnp.bfloat16)


def shard_levels(key, dims, cuts, low, top_value):
    factor_of = 1.0
    for dim, blocks in cuts:
        steps = jax.random.uniform(jax.random.fold_in(jax.random.fold_in(key, 6), dim), (blocks,), jnp.float32, low / len(cuts), top_value / len(cuts))
        factor_of = factor_of * jnp.repeat(jnp.exp(steps), dims[dim] // blocks).reshape((-1,) + (1,) * (len(dims) - 1 - dim))
    return factor_of


def profile(number_of, total, limit, lean):
    loads = [(1 << 20) // math.isqrt(grade ** lean) + 1 for grade in range(2, number_of + 1)]
    surplus, holding = total - limit - (number_of - 1), [1] * (number_of - 1)
    while surplus > 0:
        free = [i for i in range(number_of - 1) if holding[i] < limit]
        mass, remaining = sum([loads[i] for i in free]), surplus
        for i in free:
            addition = min(limit - holding[i], max(1, remaining * loads[i] // mass), surplus)
            holding[i] = holding[i] + addition
            surplus = surplus - addition
    return np.array([limit] + holding)


def ragged_sizes(own_key, count, total, limit, skew):
    if count == 2:
        one = jax.random.randint(own_key, (), max(1, total - limit), min(limit, total - 1) + 1)
        return jnp.stack([one, total - one])
    sizes = jnp.asarray(profile(count, total, limit, skew), jnp.int32)
    pairs = (count - 1) // 2
    source_of, sink = sizes[1:1 + 2 * pairs:2], sizes[2:2 + 2 * pairs:2]
    room = jnp.minimum(source_of - 1, limit - sink)
    passed = jax.random.randint(jax.random.fold_in(own_key, 1), (pairs,), 0, 1 << 20) % (room + 1)
    sizes = sizes.at[1:1 + 2 * pairs:2].set(source_of - passed).at[2:2 + 2 * pairs:2].set(sink + passed)
    return sizes[jax.random.permutation(jax.random.fold_in(own_key, 2), count)]


def assign_block(key, own, number, rows, amount, top, limit, slope):
    sequence = jax.random.permutation(key, amount)
    crowded, usual = shares(amount, rows * top, limit, slope, True), shares(amount, rows * top, limit, slope, False)
    places = jnp.arange(amount)

    def named(lengths, turn):
        used = int((lengths > 0).sum())
        fixed = max(1, used // 4)
        passed = fixed + (places - fixed + turn * (used - fixed)) % max(1, amount - fixed)
        return jnp.zeros((amount,), jnp.int32).at[sequence[jnp.where(places < fixed, places, passed)]].set(jnp.asarray(lengths, jnp.int32))

    lengths = jnp.where(number % 4 == 0, named(crowded, number // 4), named(usual, number - number // 4 - 1))
    mixed = jax.random.permutation(jax.random.fold_in(own, 3), amount)
    giver, taker = mixed[0:amount // 2 * 2:2], mixed[1:amount // 2 * 2:2]
    margin = jnp.minimum(lengths[giver] - 1, limit - lengths[taker]) // 2
    margin = jnp.where((giver == sequence[0]) | (taker == sequence[0]) | (lengths[taker] == 0), 0, jnp.maximum(margin, 0))
    passed = jax.random.randint(jax.random.fold_in(own, 4), (amount // 2,), 0, 1 << 20) % (margin + 1)
    lengths = lengths.at[giver].add(-passed).at[taker].add(passed)
    members = jnp.searchsorted(jnp.cumsum(lengths), jnp.arange(rows * top), side="right").astype(jnp.int32)
    listing = members.reshape(top, rows).T
    listing = listing[jax.random.permutation(jax.random.fold_in(own, 1), rows)]
    turn = jax.random.randint(jax.random.fold_in(own, 2), (rows, 1), 0, top)
    return jnp.take_along_axis(listing, (jnp.arange(top)[None, :] + turn) % top, axis=1)


def shares(count, total, most, slope, full):
    weights = [(1 << 20) // math.isqrt(grade ** slope) + 1 for grade in range(1, count + 1)]
    largest = most if full else min(most, max(-(-total // count), total * weights[0] // sum(weights)))
    least = 1 if total - largest >= count - 1 else 0
    given, spare = [largest] + [least] * (count - 1), total - largest - least * (count - 1)
    while spare > 0:
        free = [i for i in range(1, count) if given[i] < largest] or [i for i in range(1, count) if given[i] < most]
        whole, left = sum([weights[i] for i in free]), spare
        for i in free:
            addition = min(most - given[i], max(1, left * weights[i] // whole), spare)
            given[i] = given[i] + addition
            spare = spare - addition
    return np.array(given)


def scatter_about(stream_key, shape, scale, limit, cuts=(), kind=jnp.bfloat16):
    level = shard_levels(stream_key, shape, cuts, -0.22, 0.18) if cuts else 1.0
    values = jax.random.normal(stream_key, shape, jnp.float32) * scale * level
    return jnp.minimum(jnp.maximum(values, -limit), limit).astype(kind)


def setup_inputs(seed: int = 0) -> dict:
    splits = jax.random.split(jax.random.key(seed), 15)
    tokens = scatter_about(splits[0], (BATCH, SEQ, D), 1.0, 6.0, ((0, 2), (1, 16)))
    queries = draw_queries(jax.random.fold_in(splits[14], 71), 0)
    kv_weight = scatter_about(splits[2], (D, LAT + ROPE), D ** -0.5, 0.125, ((0, 8),))
    kv_gain = jnp.clip(1.0 + 0.1 * jax.random.normal(splits[3], (LAT,), jnp.float32), 0.5, 1.5).astype(jnp.bfloat16)
    uv_weight = scatter_about(splits[4], (HEADS, LAT, VH), (LAT // 8) ** -0.5, 0.75, ((0, 8),))
    out_weight = scatter_about(splits[5], (HEADS * VH, D), VH ** -0.5, 0.5, ((0, 8),))
    post_gain = jnp.clip(1.0 + 0.1 * jax.random.normal(splits[6], (D,), jnp.float32), 0.5, 1.5).astype(jnp.bfloat16)
    router_weight = scatter_about(splits[7], (D, EXPERTS), D ** -0.5, 0.125)
    expert_ids_keys = jax.random.split(jax.random.fold_in(splits[8], 1), BATCH * SEQ // SEQ_DEV)
    expert_ids_turns = jax.random.permutation(jax.random.fold_in(splits[8], 3), BATCH * SEQ // SEQ_DEV)
    expert_ids = jax.vmap(lambda own, number: assign_block(jax.random.fold_in(splits[8], 2), own, number, SEQ_DEV, EXPERTS, TOPK, CAP, 2))(expert_ids_keys, expert_ids_turns).reshape((BATCH, SEQ, TOPK))
    doc_ids = jax.vmap(lambda own: jnp.searchsorted(jnp.cumsum(ragged_sizes(own, DOCS, SEQ, SEQ // 2, 0)), jnp.arange(SEQ), side="right"))(jax.random.split(splits[9], BATCH)).reshape((BATCH, SEQ)).astype(jnp.int32)
    gate_weight = scatter_about(splits[10], (EXPERTS, D, FFE), D ** -0.5, 0.125, ((0, 16), (2, 8)))
    up_weight = scatter_about(splits[11], (EXPERTS, D, FFE), D ** -0.5, 0.125, ((0, 16), (2, 8)))
    down_weight = scatter_about(splits[12], (EXPERTS, FFE, D), FFE ** -0.5, 0.15625, ((0, 16), (1, 8)))
    cotangent = scatter_about(splits[13], (BATCH, SEQ, D), 1.0, 6.0, ((0, 2), (1, 16)))
    return {"tokens": tokens, "queries": queries, "kv_weight": kv_weight, "kv_gain": kv_gain, "uv_weight": uv_weight, "out_weight": out_weight, "post_gain": post_gain, "router_weight": router_weight, "expert_ids": expert_ids, "doc_ids": doc_ids, "gate_weight": gate_weight, "up_weight": up_weight, "down_weight": down_weight, "cotangent": cotangent}


epsilon = 1e-06

def rms_scale(values, gain):
    return values * lax.rsqrt(lax.optimization_barrier(jnp.mean(values * values, axis=-1, keepdims=True)) + epsilon) * gain

def rotate(rope_part, positions):
    half_width = rope_part.shape[-1] // 2
    frequency = jnp.power(10000.0, -2.0 * jnp.arange(half_width, dtype=jnp.float32) / rope_part.shape[-1])
    angles = positions.astype(jnp.float32)[:, None] * frequency[None, :]
    cosine = jnp.cos(angles)
    sine_part = jnp.sin(angles)
    first_half = rope_part[:, :half_width]
    second = rope_part[:, half_width:]
    return jnp.concatenate([first_half * cosine - second * sine_part, second * cosine + first_half * sine_part], axis=1)

def attend(token_rows, query_rows, doc_rows, kv_weight, kv_gain, uv_weight, out_weight):
    compressed = jnp.dot(token_rows, kv_weight, preferred_element_type=jnp.float32)
    latent = rms_scale(compressed[:, :LAT], kv_gain.astype(jnp.float32)).astype(jnp.bfloat16)
    positions = jnp.arange(SEQ, dtype=jnp.int32)
    rope_key = rotate(compressed[:, LAT:], positions).astype(jnp.bfloat16)
    key_rows = jnp.concatenate([latent, rope_key], axis=1).astype(jnp.float32)
    latent_wide = latent.astype(jnp.float32)
    score_scale = (NOPE + ROPE) ** (-0.5)

    def block(first_row):
        query_block = lax.dynamic_slice_in_dim(query_rows, first_row, SEQ_DEV, 0).astype(jnp.float32)
        query_pos = first_row + jnp.arange(SEQ_DEV, dtype=jnp.int32)
        query_doc = lax.dynamic_slice_in_dim(doc_rows, first_row, SEQ_DEV, 0)
        scores = jnp.einsum('qhd,kd->qhk', query_block, key_rows) * score_scale
        allowed = (positions[None, :] <= query_pos[:, None]) & (doc_rows[None, :] == query_doc[:, None])
        allowed = allowed[:, None, :]
        score_peak = lax.optimization_barrier(jnp.max(jnp.where(allowed, scores, -1e+30), axis=-1, keepdims=True))
        weights = jnp.exp(jnp.where(allowed, scores - score_peak, -1e+30))
        weight_total = lax.optimization_barrier(jnp.sum(weights, axis=-1, keepdims=True))
        rounded = lax.optimization_barrier(weights.astype(jnp.bfloat16))
        mixed_latent = jnp.einsum('qhk,kl->qhl', rounded.astype(jnp.float32), latent_wide) / weight_total
        return mixed_latent.astype(jnp.bfloat16)
    starts = jnp.arange(SEQ // SEQ_DEV, dtype=jnp.int32) * SEQ_DEV
    mixed_latent = lax.map(block, starts).reshape(SEQ, HEADS, LAT)
    mixed_latent = lax.optimization_barrier(mixed_latent)
    head_values = jnp.einsum('qhl,hlv->qhv', mixed_latent.astype(jnp.float32), uv_weight.astype(jnp.float32))
    head_values = head_values.astype(jnp.bfloat16).reshape(SEQ, HEADS * VH)
    return jnp.dot(head_values, out_weight, preferred_element_type=jnp.float32)

def reference(tokens, queries, kv_weight, kv_gain, uv_weight, out_weight, post_gain, router_weight, expert_ids, doc_ids, gate_weight, up_weight, down_weight, cotangent):
    attention = jnp.stack([attend(tokens[batch_row], queries[batch_row], doc_ids[batch_row], kv_weight, kv_gain, uv_weight, out_weight) for batch_row in range(BATCH)])
    hidden = (tokens.astype(jnp.float32) + attention).astype(jnp.bfloat16)
    normed = rms_scale(hidden.astype(jnp.float32), post_gain.astype(jnp.float32)).astype(jnp.bfloat16)
    flat_rows = normed.reshape(-1, D)
    logits = jnp.dot(flat_rows, router_weight, preferred_element_type=jnp.float32)
    router_probs = jax.nn.softmax(logits, axis=-1)
    flat_ids = expert_ids.reshape(-1, TOPK).astype(jnp.int32)
    chosen = jnp.take_along_axis(router_probs, flat_ids, axis=1)
    chosen_sum = lax.optimization_barrier(jnp.sum(chosen, axis=1, keepdims=True))
    route_w = chosen / chosen_sum
    route_wb = route_w.astype(jnp.bfloat16)
    blocks = BATCH * N_CTX
    block_ids = flat_ids.reshape(blocks, SEQ_DEV * TOPK)
    onehot = (block_ids[:, :, None] == jnp.arange(EXPERTS, dtype=jnp.int32)[None, None, :]).astype(jnp.int32)
    slot_rank = lax.optimization_barrier(jnp.sum((jnp.cumsum(onehot, axis=1) - onehot) * onehot, axis=2))
    slot_index = (block_ids * CAP + slot_rank).reshape(blocks, SEQ_DEV, TOPK)
    block_axis = jnp.arange(blocks, dtype=jnp.int32)[:, None, None]
    row_copies = jnp.broadcast_to(flat_rows.reshape(blocks, SEQ_DEV, 1, D), (blocks, SEQ_DEV, TOPK, D))
    outgoing = jnp.zeros((blocks, EXPERTS * CAP, D), jnp.bfloat16).at[block_axis, slot_index].set(row_copies)
    cot_rows = cotangent.reshape(blocks, SEQ_DEV, 1, D).astype(jnp.float32)
    weighted_cot = (route_wb.astype(jnp.float32).reshape(blocks, SEQ_DEV, TOPK, 1) * cot_rows).astype(jnp.bfloat16)
    slot_cot = jnp.zeros((blocks, EXPERTS * CAP, D), jnp.bfloat16).at[block_axis, slot_index].set(weighted_cot)
    expert_inputs = outgoing.reshape(blocks, EXPERTS, CAP, D).transpose(1, 0, 2, 3)
    expert_cots = slot_cot.reshape(blocks, EXPERTS, CAP, D).transpose(1, 0, 2, 3)
    slice_width = FFE // N_EXP

    def expert(operands):
        inputs, cots, gate_one, up_one, down_one = operands
        input_rows = inputs.reshape(-1, D)
        gate_pre = jnp.dot(input_rows, gate_one, preferred_element_type=jnp.float32)
        up_pre = jnp.dot(input_rows, up_one, preferred_element_type=jnp.float32)
        activated = lax.optimization_barrier((jax.nn.silu(gate_pre) * up_pre).astype(jnp.bfloat16))
        parts = jnp.einsum('rjf,jfd->jrd', activated.astype(jnp.float32).reshape(-1, N_EXP, slice_width), down_one.astype(jnp.float32).reshape(N_EXP, slice_width, D))
        parts = lax.optimization_barrier(parts.astype(jnp.bfloat16))
        expert_out = lax.optimization_barrier(jnp.sum(parts.astype(jnp.float32), axis=0))
        cot_slots = cots.reshape(-1, D)
        down_grad = jnp.dot(activated.T, cot_slots, preferred_element_type=jnp.float32)
        dact = jnp.dot(cot_slots, down_one.T, preferred_element_type=jnp.float32)
        sigmoid_gate = jax.nn.sigmoid(gate_pre)
        dgate = (dact * up_pre * sigmoid_gate * (1.0 + gate_pre * (1.0 - sigmoid_gate))).astype(jnp.bfloat16)
        dup = (dact * gate_pre * sigmoid_gate).astype(jnp.bfloat16)
        gate_grad = jnp.dot(input_rows.T, dgate, preferred_element_type=jnp.float32)
        up_grad = jnp.dot(input_rows.T, dup, preferred_element_type=jnp.float32)
        return (expert_out.reshape(blocks, CAP, D), gate_grad.astype(jnp.bfloat16), up_grad.astype(jnp.bfloat16), down_grad.astype(jnp.bfloat16))
    expert_out, gate_grad, up_grad, down_grad = lax.map(expert, (expert_inputs, expert_cots, gate_weight, up_weight, down_weight))
    block_out = expert_out.transpose(1, 0, 2, 3).reshape(blocks, EXPERTS * CAP, D)
    picked = block_out[block_axis, slot_index].reshape(-1, TOPK, D)
    moe = lax.optimization_barrier(jnp.sum(route_wb.astype(jnp.float32)[:, :, None] * picked, axis=1))
    layer_out = (hidden.astype(jnp.float32) + moe.reshape(BATCH, SEQ, D)).astype(jnp.bfloat16)
    cot_flat = cotangent.reshape(-1, D).astype(jnp.float32)
    dweight = lax.optimization_barrier(jnp.sum(cot_flat[:, None, :] * picked, axis=2))
    mean_term = lax.optimization_barrier(jnp.sum(dweight * route_w, axis=1, keepdims=True))
    dchosen = (dweight - mean_term) / chosen_sum
    id_hits = (flat_ids[:, :, None] == jnp.arange(EXPERTS, dtype=jnp.int32)[None, None, :]).astype(jnp.float32)
    dprobs = lax.optimization_barrier(jnp.sum(id_hits * dchosen[:, :, None], axis=1))
    dlogits = router_probs * (dprobs - lax.optimization_barrier(jnp.sum(router_probs * dprobs, axis=1, keepdims=True)))
    router_grad = jnp.dot(flat_rows.astype(jnp.float32).T, dlogits, precision=lax.Precision.HIGHEST)
    return (layer_out, router_grad, gate_grad, up_grad, down_grad)
```

```python
import jax
import jax.numpy as jnp
import numpy as np
from jax import lax
from jax.sharding import PartitionSpec as P

ROPE = 64
NOPE = 128
DOCS = 4
epsilon = 1e-06
BF = jnp.bfloat16
F32 = jnp.float32


def swap(array, axis):
    return lax.all_to_all(array, axis, split_axis=0, concat_axis=0, tiled=True)


def spread(array, axis):
    count = lax.axis_size(axis)
    return swap(jnp.broadcast_to(array[None], (count, *array.shape)), axis)


def partner(array, axis):
    count = lax.axis_size(axis)
    return lax.ppermute(array, axis, [(i, i ^ 1) for i in range(count)])


def rms_scale(values, gain):
    return values * lax.rsqrt(jnp.mean(values * values, axis=-1, keepdims=True) + epsilon) * gain


def rotate(rope_part, positions):
    half_width = rope_part.shape[-1] // 2
    frequency = jnp.power(
        10000.0, -2.0 * jnp.arange(half_width, dtype=F32) / rope_part.shape[-1]
    )
    angles = positions.astype(F32)[:, None] * frequency[None, :]
    cosine = jnp.cos(angles)
    sine_part = jnp.sin(angles)
    first_half = rope_part[:, :half_width]
    second = rope_part[:, half_width:]
    return jnp.concatenate(
        [first_half * cosine - second * sine_part, second * cosine + first_half * sine_part], axis=1
    )


def dot32(a, b):
    return jnp.dot(a, b, preferred_element_type=F32)


def ein32(spec, a, b):
    return jnp.einsum(spec, a, b, preferred_element_type=F32)


def local(
    tokens,
    queries,
    kv_weight,
    kv_gain,
    uv_weight,
    out_weight,
    post_gain,
    router_weight,
    expert_ids,
    doc_ids,
    gate_weight,
    up_weight,
    down_weight,
    cotangent,
):
    rows = tokens[0]
    cot_rows = cotangent[0]
    ids = expert_ids[0]
    docs = doc_ids[0]
    n_rows, width = rows.shape
    latent_width = kv_gain.shape[0]
    n_exp = lax.axis_size("exp")
    n_ctx = lax.axis_size("ctx")
    me = lax.axis_index("exp")
    col, par = me // 2, me % 2
    block = lax.axis_index("ctx")
    core = lax.axis_index("dp")
    experts = router_weight.shape[1]
    held = experts // n_ctx
    cap = 32
    quarter = held * cap // n_exp
    per = cap // quarter
    heads = queries.shape[2]

    expert_of = jnp.arange(experts, dtype=jnp.int32)
    hit = jnp.any(ids.T[None, :, :] == expert_of[:, None, None], axis=1)
    before = jnp.asarray(np.triu(np.ones((n_rows, n_rows)), 1), BF)
    rank = dot32(hit.astype(BF), before).astype(jnp.int32)
    rank = jnp.where(hit, rank, -1)
    slots = rank[:, None, :] == jnp.arange(cap, dtype=jnp.int32)[None, :, None]
    mine = rank.reshape(n_ctx, held, n_rows)
    mine = jnp.where(me // per == 0, mine[:, 0], mine[:, 1])
    pick = mine[:, None, :] == (
        (me % per) * quarter + jnp.arange(quarter, dtype=jnp.int32)[None, :, None]
    )
    pick = pick.astype(BF).reshape(n_ctx * quarter, n_rows)

    def dispatch(values):
        out = dot32(pick, values).astype(BF).reshape(n_ctx, quarter, width)
        out = swap(out, "ctx").reshape(n_ctx * quarter, width)
        return spread(out, "exp").reshape(held, per * n_ctx * quarter, width)

    share = n_rows // n_exp
    kv_rows = kv_weight.shape[0]
    columns = lax.dynamic_slice_in_dim(rows, me * kv_rows, kv_rows, 1)
    part = dot32(columns, kv_weight).reshape(n_exp, share, -1)
    compressed = jnp.sum(swap(part, "exp"), axis=0)
    positions = block * n_rows + me * share + jnp.arange(share, dtype=jnp.int32)
    latent = rms_scale(compressed[:, :latent_width], kv_gain.astype(F32)).astype(BF)
    rope_key = rotate(compressed[:, latent_width:], positions).astype(BF)
    docs_share = lax.dynamic_slice_in_dim(docs, me * share, share, 0)
    doc_of = jnp.arange(64, dtype=jnp.int32)
    doc_key = (docs_share[:, None] == doc_of[None, :]).astype(BF)
    keys = jnp.concatenate([latent, rope_key, doc_key], axis=1)
    keys = spread(spread(keys, "ctx").reshape(n_ctx * share, -1), "exp")
    keys = keys.reshape(n_exp * n_ctx * share, -1)
    key_at = np.arange(n_exp * n_ctx * share, dtype=np.int32).reshape(n_exp, n_ctx, share)
    key_at = (
        (key_at // share % n_ctx) * n_rows + (key_at // (share * n_ctx)) * share + key_at % share
    ).reshape(-1)

    cots = dispatch(cot_rows)
    down_cols = down_weight.reshape(held, -1, n_exp // 2, 2 * width // n_exp)
    down_cols = jnp.transpose(down_cols, (2, 0, 1, 3)).reshape(n_exp, -1, 2 * width // n_exp)
    down_cols = swap(down_cols, "exp")

    differs = (doc_of[None, :] < DOCS) & (docs[:, None] != doc_of[None, :])
    doc_query = jnp.where(differs, -1e30, 0.0).astype(BF)
    query = jnp.concatenate(
        [
            jnp.transpose(queries[0], (1, 0, 2)),
            jnp.broadcast_to(doc_query[None], (heads, *doc_query.shape)),
        ],
        axis=2,
    ).reshape(heads * n_rows, -1)
    query_at = block * n_rows + jnp.arange(n_rows, dtype=jnp.int32)
    score_scale = (NOPE + ROPE) ** (-0.5)
    scores = ein32("qd,kd->qk", query, keys).reshape(heads, n_rows, -1)
    reached = (jnp.asarray(key_at)[None, :] <= query_at[:, None])[None]
    scores = jnp.where(reached, scores * score_scale, -1e30)
    weights = jnp.exp(scores - jnp.max(scores, axis=-1, keepdims=True))
    total = jnp.sum(weights, axis=-1, keepdims=True)
    mixed = (ein32("hqk,kl->hql", weights.astype(BF), keys[:, :latent_width]) / total).astype(BF)
    head_values = jnp.concatenate(
        [dot32(mixed[h], uv_weight[h]).astype(BF) for h in range(heads)], axis=1
    )
    part = dot32(head_values, out_weight).astype(BF).reshape(n_exp, share, width)
    attention = jnp.sum(swap(part, "exp").astype(F32), axis=0)
    own_rows = lax.dynamic_slice_in_dim(rows, me * share, share, 0).astype(F32)
    hidden = spread((own_rows + attention).astype(BF), "exp").reshape(n_rows, width)
    normed = rms_scale(hidden.astype(F32), post_gain.astype(F32)).astype(BF)
    arrived = dispatch(normed)

    logits = lax.dot_general(
        router_weight, normed, (((0,), (1,)), ((), ())), preferred_element_type=F32
    )
    probs = jax.nn.softmax(logits, axis=0)
    chosen = jnp.where(hit, probs, 0.0)
    chosen_sum = jnp.sum(chosen, axis=0, keepdims=True)
    route_w = chosen / chosen_sum
    route_b = route_w.astype(BF)
    slot_w = jnp.sum(jnp.where(slots, route_b.astype(F32)[:, None, :], 0.0), axis=2)
    slot_w = swap(slot_w.reshape(n_ctx, held * cap), "ctx")
    slot_w = jnp.transpose(slot_w.reshape(n_ctx, held, per, quarter), (1, 2, 0, 3))
    slot_w = slot_w.reshape(held, -1, 1)

    gate_pre = ein32("jrd,jdf->jrf", arrived, gate_weight)
    up_pre = ein32("jrd,jdf->jrf", arrived, up_weight)
    sigmoid_gate = jax.nn.sigmoid(gate_pre)
    activated = (gate_pre * sigmoid_gate * up_pre).astype(BF)
    wide = swap(
        jnp.broadcast_to(activated[None], (n_exp // held, *activated.shape)).reshape(
            n_exp, *activated.shape[1:]
        ),
        "exp",
    )
    result = ein32("frk,fkc->rc", wide, down_cols).astype(BF)
    result = jnp.transpose(result.reshape(per, n_ctx, quarter, -1), (1, 0, 2, 3))
    returned = swap(result.reshape(n_ctx, cap, -1), "ctx").reshape(n_ctx * cap, -1)

    half = n_rows // 2
    wide_cols = 2 * width // n_exp
    combine = jnp.where(slots, route_b[:, None, :], jnp.zeros((), BF))
    combine = combine.reshape(n_ctx, held, cap, n_rows)
    combine = jnp.where(par == 0, combine[:, 0], combine[:, 1]).reshape(n_ctx * cap, n_rows)
    moe = lax.dot_general(
        combine, returned, (((0,), (0,)), ((), ())), preferred_element_type=F32
    )
    kept = lax.dynamic_slice_in_dim(moe, par * half, half, 0)
    sent = lax.dynamic_slice_in_dim(moe, (1 - par) * half, half, 0)
    own_hidden = lax.dynamic_slice(hidden, (par * half, col * wide_cols), (half, wide_cols))
    out = own_hidden.astype(F32) + (kept + partner(sent, "exp"))
    out = spread(out.astype(BF), "exp").reshape(n_exp // 2, 2, half, wide_cols)
    layer_out = jnp.transpose(out, (1, 2, 0, 3)).reshape(n_rows, width)

    dact = ein32("jrd,jfd->jrf", cots, down_weight)
    dweight = jnp.sum(activated.astype(F32) * dact, axis=2)
    dweight = jnp.transpose(dweight.reshape(held, per, n_ctx, quarter), (2, 0, 1, 3))
    dweight = swap(dweight.reshape(n_ctx, held * cap), "ctx")
    dweight = jnp.sum(spread(dweight, "exp"), axis=0).reshape(experts, cap, 1)
    dact = dact * slot_w
    dgate = (dact * up_pre * sigmoid_gate * (1.0 + gate_pre * (1.0 - sigmoid_gate))).astype(BF)
    dup = (dact * gate_pre * sigmoid_gate).astype(BF)
    weighted = (activated.astype(F32) * slot_w).astype(BF)
    split = width // 2
    near, far = core * split, (1 - core) * split
    cut = lambda array, at: lax.dynamic_slice_in_dim(array, at, split, 2)
    grads = []
    for left, right, spec in (
        (arrived, dgate, "jrd,jrf->jdf"),
        (arrived, dup, "jrd,jrf->jdf"),
        (cots, weighted, "jrd,jrf->jfd"),
    ):
        other = partner(ein32(spec, cut(left, far), right).astype(BF), "dp")
        grads.append((ein32(spec, cut(left, near), right) + other.astype(F32)).astype(BF))

    dweight = jnp.sum(jnp.where(slots, dweight, 0.0), axis=1)
    mean_term = jnp.sum(dweight * route_w, axis=0, keepdims=True)
    dprobs = jnp.where(hit, (dweight - mean_term) / chosen_sum, 0.0)
    dlogits = probs * (dprobs - jnp.sum(probs * dprobs, axis=0, keepdims=True))
    normed_cols = lax.dynamic_slice_in_dim(normed, me * (width // n_exp), width // n_exp, 1)
    term = jnp.dot(dlogits, normed_cols.astype(F32), precision=lax.Precision.HIGHEST)
    term = term + partner(term, "dp")
    term = jnp.sum(spread(term, "ctx"), axis=0)
    router_grad = jnp.transpose(spread(term, "exp"), (0, 2, 1)).reshape(width, experts)
    return (layer_out[None], router_grad, *grads)


def solution(mesh):
    placed = (
        P("dp", "ctx", None),
        P("dp", "ctx", "exp", None),
        P("exp", None),
        P(),
        P("exp", None, None),
        P("exp", None),
        P(),
        P(),
        P("dp", "ctx", None),
        P("dp", "ctx"),
        P("ctx", None, "exp"),
        P("ctx", None, "exp"),
        P("ctx", "exp", None),
        P("dp", "ctx", None),
    )
    return jax.shard_map(
        local,
        mesh=mesh,
        in_specs=placed,
        out_specs=(
            P("dp", "ctx", None),
            P(),
            P("ctx", "dp", "exp"),
            P("ctx", "dp", "exp"),
            P("ctx", "exp", "dp"),
        ),
        check_vma=False,
    )
```

```python
import jax
import jax.numpy as jnp
import numpy as np
from jax import lax
from jax.sharding import PartitionSpec as P

ROPE = 64
NOPE = 128
DOCS = 4
epsilon = 1e-06
BF = jnp.bfloat16
F32 = jnp.float32


def swap(array, axis):
    return lax.all_to_all(array, axis, split_axis=0, concat_axis=0, tiled=True)


def spread(array, axis):
    count = lax.axis_size(axis)
    return swap(jnp.broadcast_to(array[None], (count, *array.shape)), axis)


def partner(array, axis):
    count = lax.axis_size(axis)
    return lax.ppermute(array, axis, [(i, i ^ 1) for i in range(count)])


def ringed(array, step):
    count = lax.axis_size("exp")
    return lax.ppermute(array, "exp", [(i, (i + step) % count) for i in range(count)])


def first_hop(array):
    return [array, ringed(array, 2), ringed(array, -2), partner(array, "exp")]


def second_hop(pieces):
    _, left, right, pair = pieces
    return [*pieces, ringed(left, 2), partner(left, "exp"), ringed(pair, -2)]


def third_hop(pieces):
    far, left_pair, right_pair = pieces[4:]
    third = far.shape[0] // 24 * 8
    return [
        *pieces,
        ringed(left_pair[:third], 2),
        ringed(right_pair[third : 2 * third], -2),
        partner(far[2 * third :], "exp"),
    ]


def gathered(array):
    return third_hop(second_hop(first_hop(array)))


def in_order(pieces):
    count = lax.axis_size("exp")
    me = lax.axis_index("exp")
    left, right, far = (me + count - 2) % count, (me + 2) % count, (me + 4) % count
    owners = [me, left, right, me ^ 1, far, left ^ 1, right ^ 1, far ^ 1, far ^ 1, far ^ 1]
    third = pieces[7].shape[0]
    starts = [0] * 8 + [third, 2 * third]
    out = jnp.zeros((count, *pieces[0].shape), pieces[0].dtype)
    for piece, owner, start in zip(pieces, owners, starts, strict=True):
        out = lax.dynamic_update_slice(out, piece[None], (owner, start, 0))
    return out


def summed(array, axis):
    count = lax.axis_size(axis)
    bit = 1
    while bit < count:
        array = array + lax.ppermute(array, axis, [(i, i ^ bit) for i in range(count)])
        bit *= 2
    return array


def halves(values, lanes):
    upper = lax.reduce_precision(values, exponent_bits=8, mantissa_bits=7)
    lane = jnp.arange(lanes, dtype=jnp.int32)
    return jnp.where(lane == 0, upper, jnp.where(lane == 1, values - upper, 0.0)).astype(BF)


def rms_scale(values, gain):
    return values * lax.rsqrt(jnp.mean(values * values, axis=-1, keepdims=True) + epsilon) * gain


def rotate(rope_part, positions):
    half_width = rope_part.shape[-1] // 2
    frequency = jnp.power(
        10000.0, -2.0 * jnp.arange(half_width, dtype=F32) / rope_part.shape[-1]
    )
    angles = positions.astype(F32)[:, None] * frequency[None, :]
    cosine = jnp.cos(angles)
    sine_part = jnp.sin(angles)
    first_half = rope_part[:, :half_width]
    second = rope_part[:, half_width:]
    return jnp.concatenate(
        [first_half * cosine - second * sine_part, second * cosine + first_half * sine_part], axis=1
    )


def dot32(a, b):
    return jnp.dot(a, b, preferred_element_type=F32)


def ein32(spec, a, b):
    return jnp.einsum(spec, a, b, preferred_element_type=F32)


def local(
    tokens,
    queries,
    kv_weight,
    kv_gain,
    uv_weight,
    out_weight,
    post_gain,
    router_weight,
    expert_ids,
    doc_ids,
    gate_weight,
    up_weight,
    down_weight,
    cotangent,
):
    rows = tokens[0]
    cot_rows = cotangent[0]
    ids = expert_ids[0]
    docs = doc_ids[0]
    n_rows, width = rows.shape
    latent_width = kv_gain.shape[0]
    n_exp = lax.axis_size("exp")
    n_ctx = lax.axis_size("ctx")
    me = lax.axis_index("exp")
    col, par = me // 2, me % 2
    block = lax.axis_index("ctx")
    core = lax.axis_index("dp")
    experts = router_weight.shape[1]
    held = experts // n_ctx
    cap = 32
    quarter = held * cap // n_exp
    per = cap // quarter
    heads = queries.shape[2]

    expert_of = jnp.arange(experts, dtype=jnp.int32)
    hit = jnp.any(ids.T[None, :, :] == expert_of[:, None, None], axis=1)
    before = jnp.asarray(np.triu(np.ones((n_rows, n_rows)), 1), BF)
    rank = dot32(hit.astype(BF), before).astype(jnp.int32)
    rank = jnp.where(hit, rank, -1)
    slots = rank[:, None, :] == jnp.arange(cap, dtype=jnp.int32)[None, :, None]
    mine = rank.reshape(n_ctx, held, n_rows)
    mine = jnp.where(me // per == 0, mine[:, 0], mine[:, 1])
    pick = mine[:, None, :] == (
        (me % per) * quarter + jnp.arange(quarter, dtype=jnp.int32)[None, :, None]
    )
    pick = pick.astype(BF).reshape(n_ctx * quarter, n_rows)

    def dispatch(values):
        out = dot32(pick, values).astype(BF).reshape(n_ctx, quarter, width)
        return swap(out, "ctx").reshape(n_ctx * quarter, width)

    def shared(out):
        return in_order(out).reshape(held, per * n_ctx * quarter, width)

    share = n_rows // n_exp
    kv_rows = kv_weight.shape[0]
    columns = lax.dynamic_slice_in_dim(rows, me * kv_rows, kv_rows, 1)
    part = dot32(columns, kv_weight).reshape(n_exp, share, -1)
    compressed = jnp.sum(swap(part, "exp"), axis=0)
    positions = block * n_rows + me * share + jnp.arange(share, dtype=jnp.int32)
    latent = rms_scale(compressed[:, :latent_width], kv_gain.astype(F32)).astype(BF)
    rope_key = rotate(compressed[:, latent_width:], positions).astype(BF)
    docs_share = lax.dynamic_slice_in_dim(docs, me * share, share, 0)
    doc_of = jnp.arange(64, dtype=jnp.int32)
    doc_key = (docs_share[:, None] == doc_of[None, :]).astype(BF)
    keys = jnp.concatenate([latent, rope_key, doc_key], axis=1)
    keys = spread(keys, "ctx").reshape(n_ctx * share, -1)
    pieces = gathered(keys)
    keys = jnp.concatenate(pieces, axis=0)
    left, right, far = (me + n_exp - 2) % n_exp, (me + 2) % n_exp, (me + 4) % n_exp
    owner = jnp.stack([me, left, right, me ^ 1, far, left ^ 1, right ^ 1, far ^ 1])
    in_block = np.arange(n_ctx * share, dtype=np.int32)
    in_block = in_block // share * n_rows + in_block % share
    key_at = (owner[:, None] * share + jnp.asarray(in_block)[None, :]).reshape(1, -1)

    cots = shared(gathered(dispatch(cot_rows)))
    wide_cols = 2 * width // n_exp
    units = gate_weight.shape[2]

    differs = (doc_of[None, :] < DOCS) & (docs[:, None] != doc_of[None, :])
    doc_query = jnp.where(differs, -1e30, 0.0).astype(BF)
    query = jnp.concatenate(
        [
            jnp.transpose(queries[0], (1, 0, 2)),
            jnp.broadcast_to(doc_query[None], (heads, *doc_query.shape)),
        ],
        axis=2,
    ).reshape(heads * n_rows, -1)
    query_at = block * n_rows + jnp.arange(n_rows, dtype=jnp.int32)
    score_scale = (NOPE + ROPE) ** (-0.5)
    scores = ein32("qd,kd->qk", query, keys).reshape(heads, n_rows, -1)
    reached = (key_at <= query_at[:, None])[None]
    scores = jnp.where(reached, scores * score_scale, -1e30)
    weights = jnp.exp(scores - jnp.max(scores, axis=-1, keepdims=True))
    total = jnp.sum(weights, axis=-1, keepdims=True)
    mixed = (ein32("hqk,kl->hql", weights.astype(BF), keys[:, :latent_width]) / total).astype(BF)
    head_values = jnp.concatenate(
        [dot32(mixed[h], uv_weight[h]).astype(BF) for h in range(heads)], axis=1
    )
    part = dot32(head_values, out_weight).astype(BF).reshape(n_exp, share, width)
    attention = jnp.sum(swap(part, "exp").astype(F32), axis=0)
    own_rows = lax.dynamic_slice_in_dim(rows, me * share, share, 0).astype(F32)
    hidden = spread((own_rows + attention).astype(BF), "exp")
    hidden = hidden.reshape(n_rows, width)
    normed = rms_scale(hidden.astype(F32), post_gain.astype(F32)).astype(BF)
    arrived = dispatch(normed)

    logits = lax.dot_general(
        router_weight, normed, (((0,), (1,)), ((), ())), preferred_element_type=F32
    )
    probs = jax.nn.softmax(logits, axis=0)
    chosen = jnp.where(hit, probs, 0.0)
    chosen_sum = jnp.sum(chosen, axis=0, keepdims=True)
    route_w = chosen / chosen_sum
    route_b = route_w.astype(BF)
    slot_w = jnp.sum(jnp.where(slots, route_b.astype(F32)[:, None, :], 0.0), axis=2)
    slot_w = slot_w.reshape(n_ctx, held * cap)
    arrived = first_hop(arrived)
    down_cols = lax.dynamic_slice_in_dim(down_weight, core * (units // 2), units // 2, 1)
    down_cols = down_cols.reshape(held, units // 2, per, wide_cols)
    arrived, slot_w, down_cols = lax.optimization_barrier((arrived, slot_w, down_cols))
    arrived = third_hop(second_hop(arrived))
    slot_w = swap(slot_w, "ctx")
    down_cols = jnp.transpose(down_cols, (2, 0, 1, 3)).reshape(n_exp, units // 2, wide_cols)
    down_cols = swap(down_cols, "exp")
    down_other = partner(down_cols, "dp")
    down_cols = jnp.concatenate(
        [
            jnp.where(core == 0, down_cols, down_other),
            jnp.where(core == 0, down_other, down_cols),
        ],
        axis=1,
    )
    slot_w = jnp.transpose(slot_w.reshape(n_ctx, held, per, quarter), (1, 2, 0, 3))
    slot_w = slot_w.reshape(held, -1, 1)
    dact = ein32("jrd,jfd->jrf", cots, down_weight)
    arrived[7], arrived[8], arrived[9], slot_w = lax.optimization_barrier(
        (*arrived[7:], slot_w)
    )
    arrived = shared(arrived)

    gate_pre = ein32("jrd,jdf->jrf", arrived, gate_weight)
    up_pre = ein32("jrd,jdf->jrf", arrived, up_weight)
    sigmoid_gate = jax.nn.sigmoid(gate_pre)
    activated = (gate_pre * sigmoid_gate * up_pre).astype(BF)
    dweight = jnp.sum(activated.astype(F32) * dact, axis=2, keepdims=True)
    wide = jnp.concatenate([activated, halves(dweight, 16)], axis=2)
    wide = jnp.broadcast_to(wide[None], (n_exp // held, *wide.shape))
    wide = swap(wide.reshape(n_exp, *wide.shape[2:]), "exp")
    dact = dact * slot_w
    dgate = (dact * up_pre * sigmoid_gate * (1.0 + gate_pre * (1.0 - sigmoid_gate))).astype(BF)
    dup = (dact * gate_pre * sigmoid_gate).astype(BF)
    weighted = (activated.astype(F32) * slot_w).astype(BF)
    split = width // 2
    near, far = core * split, (1 - core) * split
    cut = lambda array, at: lax.dynamic_slice_in_dim(array, at, split, 2)
    terms = (
        (arrived, dgate, "jrd,jrf->jdf"),
        (arrived, dup, "jrd,jrf->jdf"),
        (cots, weighted, "jrd,jrf->jfd"),
    )
    away = [ein32(spec, cut(left, far), right).astype(BF) for left, right, spec in terms]
    wide, away = lax.optimization_barrier((wide, away))
    away = [partner(array, "dp") for array in away]
    dweight = jnp.sum(jnp.sum(wide[:, :, units:].astype(F32), axis=2), axis=0)[:, None]
    wide = wide[:, :, :units]
    result = ein32("frk,fkc->rc", wide, down_cols).astype(BF)
    result = jnp.concatenate([result, halves(dweight, 128)], axis=1)
    result = jnp.transpose(result.reshape(per, n_ctx, quarter, -1), (1, 0, 2, 3))
    returned = swap(result.reshape(n_ctx, cap, -1), "ctx").reshape(n_ctx * cap, -1)
    grads = [
        (ein32(spec, cut(left, near), right) + other.astype(F32)).astype(BF)
        for (left, right, spec), other in zip(terms, away, strict=True)
    ]
    returned, grads = lax.optimization_barrier((returned, grads))
    dweight = jnp.sum(returned[:, wide_cols:].astype(F32), axis=1).reshape(n_ctx, cap, 1)
    returned = returned[:, :wide_cols]

    half = n_rows // 2
    combine = jnp.where(slots, route_b[:, None, :], jnp.zeros((), BF))
    combine = combine.reshape(n_ctx, held, cap, n_rows)
    combine = jnp.where(par == 0, combine[:, 0], combine[:, 1]).reshape(n_ctx * cap, n_rows)
    moe = lax.dot_general(
        combine, returned, (((0,), (0,)), ((), ())), preferred_element_type=F32
    )
    kept = lax.dynamic_slice_in_dim(moe, par * half, half, 0)
    sent = lax.dynamic_slice_in_dim(moe, (1 - par) * half, half, 0)
    own_hidden = lax.dynamic_slice(hidden, (par * half, col * wide_cols), (half, wide_cols))
    held_slots = slots.reshape(n_ctx, held, cap, n_rows)
    held_slots = jnp.where(par == 0, held_slots[:, 0], held_slots[:, 1])
    dweight = jnp.sum(jnp.where(held_slots, dweight, 0.0), axis=1)
    beside = jnp.pad(dweight, ((0, 0), (0, wide_cols - n_rows)))
    theirs = partner(jnp.concatenate([sent, beside], axis=0), "exp")
    out = own_hidden.astype(F32) + (kept + theirs[:half])
    theirs = theirs[half:, :n_rows]
    gathered_out = spread(out.astype(BF), "exp")
    out = gathered_out.reshape(n_exp // 2, 2, half, wide_cols)
    layer_out = jnp.transpose(out, (1, 2, 0, 3)).reshape(n_rows, width)

    dweight = jnp.stack(
        [jnp.where(par == 0, dweight, theirs), jnp.where(par == 0, theirs, dweight)], axis=1
    ).reshape(experts, n_rows)
    mean_term = jnp.sum(dweight * route_w, axis=0, keepdims=True)
    dprobs = jnp.where(hit, (dweight - mean_term) / chosen_sum, 0.0)
    dlogits = probs * (dprobs - jnp.sum(probs * dprobs, axis=0, keepdims=True))
    normed_cols = lax.dynamic_slice_in_dim(normed, me * (width // n_exp), width // n_exp, 1)
    term = jnp.dot(dlogits, normed_cols.astype(F32), precision=lax.Precision.HIGHEST)
    term = summed(summed(term, "dp"), "ctx")
    term, _ = lax.optimization_barrier((term, gathered_out))
    router_grad = jnp.transpose(spread(term, "exp"), (0, 2, 1)).reshape(width, experts)
    return (layer_out[None], router_grad, *grads)


def solution(mesh):
    placed = (
        P("dp", "ctx", None),
        P("dp", "ctx", "exp", None),
        P("exp", None),
        P(),
        P("exp", None, None),
        P("exp", None),
        P(),
        P(),
        P("dp", "ctx", None),
        P("dp", "ctx"),
        P("ctx", None, "exp"),
        P("ctx", None, "exp"),
        P("ctx", "exp", None),
        P("dp", "ctx", None),
    )
    return jax.shard_map(
        local,
        mesh=mesh,
        in_specs=placed,
        out_specs=(
            P("dp", "ctx", None),
            P(),
            P("ctx", "dp", "exp"),
            P("ctx", "dp", "exp"),
            P("ctx", "exp", "dp"),
        ),
        check_vma=False,
    )
```

```python
import jax
import jax.numpy as jnp
import numpy as np
from jax import lax
from jax.sharding import PartitionSpec as P

ROPE = 64
NOPE = 128
DOCS = 4
epsilon = 1e-06
BF = jnp.bfloat16
F32 = jnp.float32


def swap(array, axis):
    return lax.all_to_all(array, axis, split_axis=0, concat_axis=0, tiled=True)


def spread(array, axis):
    count = lax.axis_size(axis)
    return swap(jnp.broadcast_to(array[None], (count, *array.shape)), axis)


def partner(array, axis):
    count = lax.axis_size(axis)
    return lax.ppermute(array, axis, [(i, i ^ 1) for i in range(count)])


def ringed(array, step):
    count = lax.axis_size("exp")
    return lax.ppermute(array, "exp", [(i, (i + step) % count) for i in range(count)])


def first_hop(array):
    return [array, ringed(array, 2), ringed(array, -2), partner(array, "exp")]


def second_hop(pieces):
    _, left, right, pair = pieces
    return [*pieces, ringed(left, 2), partner(left, "exp"), ringed(pair, -2)]


def third_hop(pieces):
    return [*pieces, partner(pieces[4], "exp")]


def gathered(array):
    return third_hop(second_hop(first_hop(array)))


def in_order(pieces):
    count = lax.axis_size("exp")
    me = lax.axis_index("exp")
    left, right, far = (me + count - 2) % count, (me + 2) % count, (me + 4) % count
    owners = [me, left, right, me ^ 1, far, left ^ 1, right ^ 1, far ^ 1]
    out = jnp.zeros((count, *pieces[0].shape), pieces[0].dtype)
    for piece, owner in zip(pieces, owners, strict=True):
        out = lax.dynamic_update_slice(out, piece[None], (owner, 0, 0))
    return out


def summed(array):
    count = lax.axis_size("ctx")
    for stride, block in ((1, 4), (4, 16)):
        moved = [
            lax.ppermute(
                array,
                "ctx",
                [(i, i // block * block + (i + k * stride) % block) for i in range(count)],
            )
            for k in (1, 2, 3)
        ]
        array = (array + moved[1]) + (moved[0] + moved[2])
    return array


def halves(values, lanes):
    upper = lax.reduce_precision(values, exponent_bits=8, mantissa_bits=7)
    lane = jnp.arange(lanes, dtype=jnp.int32)
    return jnp.where(lane == 0, upper, jnp.where(lane == 1, values - upper, 0.0)).astype(BF)


def rms_scale(values, gain):
    return values * lax.rsqrt(jnp.mean(values * values, axis=-1, keepdims=True) + epsilon) * gain


def rotate(rope_part, positions):
    half_width = rope_part.shape[-1] // 2
    frequency = jnp.power(
        10000.0, -2.0 * jnp.arange(half_width, dtype=F32) / rope_part.shape[-1]
    )
    angles = positions.astype(F32)[:, None] * frequency[None, :]
    cosine = jnp.cos(angles)
    sine_part = jnp.sin(angles)
    first_half = rope_part[:, :half_width]
    second = rope_part[:, half_width:]
    return jnp.concatenate(
        [first_half * cosine - second * sine_part, second * cosine + first_half * sine_part], axis=1
    )


def dot32(a, b):
    return jnp.dot(a, b, preferred_element_type=F32)


def ein32(spec, a, b):
    return jnp.einsum(spec, a, b, preferred_element_type=F32)


def local(
    tokens,
    queries,
    kv_weight,
    kv_gain,
    uv_weight,
    out_weight,
    post_gain,
    router_weight,
    expert_ids,
    doc_ids,
    gate_weight,
    up_weight,
    down_weight,
    cotangent,
):
    rows = tokens[0]
    cot_rows = cotangent[0]
    ids = expert_ids[0]
    docs = doc_ids[0]
    n_rows, width = rows.shape
    latent_width = kv_gain.shape[0]
    n_exp = lax.axis_size("exp")
    n_ctx = lax.axis_size("ctx")
    me = lax.axis_index("exp")
    col, par = me // 2, me % 2
    block = lax.axis_index("ctx")
    core = lax.axis_index("dp")
    experts = router_weight.shape[1]
    held = experts // n_ctx
    cap = 32
    quarter = held * cap // n_exp
    per = cap // quarter
    heads = queries.shape[2]

    expert_of = jnp.arange(experts, dtype=jnp.int32)
    hit = jnp.any(ids.T[None, :, :] == expert_of[:, None, None], axis=1)
    before = jnp.asarray(np.triu(np.ones((n_rows, n_rows)), 1), BF)
    rank = dot32(hit.astype(BF), before).astype(jnp.int32)
    rank = jnp.where(hit, rank, -1)
    slots = rank[:, None, :] == jnp.arange(cap, dtype=jnp.int32)[None, :, None]
    mine = rank.reshape(n_ctx, held, n_rows)
    mine = jnp.where(me // per == 0, mine[:, 0], mine[:, 1])
    pick = mine[:, None, :] == (
        (me % per) * quarter + jnp.arange(quarter, dtype=jnp.int32)[None, :, None]
    )
    pick = pick.astype(BF).reshape(n_ctx * quarter, n_rows)

    def dispatch(values):
        out = dot32(pick, values).astype(BF).reshape(n_ctx, quarter, width)
        return swap(out, "ctx").reshape(n_ctx * quarter, width)

    def shared(out):
        return in_order(out).reshape(held, per * n_ctx * quarter, width)

    share = n_rows // n_exp
    kv_rows = kv_weight.shape[0]
    columns = lax.dynamic_slice_in_dim(rows, me * kv_rows, kv_rows, 1)
    part = dot32(columns, kv_weight).reshape(n_exp, share, -1)
    compressed = jnp.sum(swap(part, "exp"), axis=0)
    positions = block * n_rows + me * share + jnp.arange(share, dtype=jnp.int32)
    latent = rms_scale(compressed[:, :latent_width], kv_gain.astype(F32)).astype(BF)
    rope_key = rotate(compressed[:, latent_width:], positions).astype(BF)
    docs_share = lax.dynamic_slice_in_dim(docs, me * share, share, 0)
    doc_of = jnp.arange(64, dtype=jnp.int32)
    doc_key = (docs_share[:, None] == doc_of[None, :]).astype(BF)
    keys = jnp.concatenate([latent, rope_key, doc_key], axis=1)
    keys = spread(keys, "ctx").reshape(n_ctx * share, -1)
    cots = dispatch(cot_rows)
    pieces = gathered(keys)
    pieces, cots = lax.optimization_barrier((pieces, cots))
    cots = shared(gathered(cots))
    wide_cols = 2 * width // n_exp
    units = gate_weight.shape[2]
    keys = jnp.concatenate(pieces, axis=0)
    left, right, far = (me + n_exp - 2) % n_exp, (me + 2) % n_exp, (me + 4) % n_exp
    owner = jnp.stack([me, left, right, me ^ 1, far, left ^ 1, right ^ 1, far ^ 1])
    in_block = np.arange(n_ctx * share, dtype=np.int32)
    in_block = in_block // share * n_rows + in_block % share
    key_at = (owner[:, None] * share + jnp.asarray(in_block)[None, :]).reshape(1, -1)

    differs = (doc_of[None, :] < DOCS) & (docs[:, None] != doc_of[None, :])
    doc_query = jnp.where(differs, -1e30, 0.0).astype(BF)
    query = jnp.concatenate(
        [
            jnp.transpose(queries[0], (1, 0, 2)),
            jnp.broadcast_to(doc_query[None], (heads, *doc_query.shape)),
        ],
        axis=2,
    ).reshape(heads * n_rows, -1)
    query_at = block * n_rows + jnp.arange(n_rows, dtype=jnp.int32)
    score_scale = (NOPE + ROPE) ** (-0.5)
    scores = ein32("qd,kd->qk", query, keys).reshape(heads, n_rows, -1)
    reached = (key_at <= query_at[:, None])[None]
    scores = jnp.where(reached, scores * score_scale, -1e30)
    weights = jnp.exp(scores - jnp.max(scores, axis=-1, keepdims=True))
    total = jnp.sum(weights, axis=-1, keepdims=True)
    mixed = (ein32("hqk,kl->hql", weights.astype(BF), keys[:, :latent_width]) / total).astype(BF)
    head_values = jnp.concatenate(
        [dot32(mixed[h], uv_weight[h]).astype(BF) for h in range(heads)], axis=1
    )
    part = dot32(head_values, out_weight).astype(BF).reshape(n_exp, share, width)
    attention = jnp.sum(swap(part, "exp").astype(F32), axis=0)
    own_rows = lax.dynamic_slice_in_dim(rows, me * share, share, 0).astype(F32)
    hidden = spread((own_rows + attention).astype(BF), "exp")
    hidden = hidden.reshape(n_rows, width)
    normed = rms_scale(hidden.astype(F32), post_gain.astype(F32)).astype(BF)
    arrived = dispatch(normed)

    logits = lax.dot_general(
        router_weight, normed, (((0,), (1,)), ((), ())), preferred_element_type=F32
    )
    probs = jax.nn.softmax(logits, axis=0)
    chosen = jnp.where(hit, probs, 0.0)
    chosen_sum = jnp.sum(chosen, axis=0, keepdims=True)
    route_w = chosen / chosen_sum
    route_b = route_w.astype(BF)
    slot_w = jnp.sum(jnp.where(slots, route_b.astype(F32)[:, None, :], 0.0), axis=2)
    slot_w = slot_w.reshape(n_ctx, held * cap)
    arrived = first_hop(arrived)
    down_cols = lax.dynamic_slice_in_dim(down_weight, core * (units // 2), units // 2, 1)
    down_cols = down_cols.reshape(held, units // 2, per, wide_cols)
    arrived, slot_w = lax.optimization_barrier((arrived, slot_w))
    arrived = second_hop(arrived)
    arrived, down_cols = lax.optimization_barrier((arrived, down_cols))
    arrived = third_hop(arrived)
    slot_w = swap(slot_w, "ctx")
    down_cols = jnp.transpose(down_cols, (2, 0, 1, 3)).reshape(n_exp, units // 2, wide_cols)
    down_cols = swap(down_cols, "exp")
    down_other = partner(down_cols, "dp")
    down_cols = jnp.concatenate(
        [
            jnp.where(core == 0, down_cols, down_other),
            jnp.where(core == 0, down_other, down_cols),
        ],
        axis=1,
    )
    slot_w = jnp.transpose(slot_w.reshape(n_ctx, held, per, quarter), (1, 2, 0, 3))
    slot_w = slot_w.reshape(held, -1, 1)
    dact = ein32("jrd,jfd->jrf", cots, down_weight)
    arrived[7], slot_w = lax.optimization_barrier((arrived[7], slot_w))
    arrived = shared(arrived)

    gate_pre = ein32("jrd,jdf->jrf", arrived, gate_weight)
    up_pre = ein32("jrd,jdf->jrf", arrived, up_weight)
    sigmoid_gate = jax.nn.sigmoid(gate_pre)
    activated = (gate_pre * sigmoid_gate * up_pre).astype(BF)
    dweight = jnp.sum(activated.astype(F32) * dact, axis=2, keepdims=True)
    wide = jnp.concatenate([activated, halves(dweight, 16)], axis=2)
    wide = jnp.broadcast_to(wide[None], (n_exp // held, *wide.shape))
    wide = swap(wide.reshape(n_exp, *wide.shape[2:]), "exp")
    dact = dact * slot_w
    dgate = (dact * up_pre * sigmoid_gate * (1.0 + gate_pre * (1.0 - sigmoid_gate))).astype(BF)
    dup = (dact * gate_pre * sigmoid_gate).astype(BF)
    weighted = (activated.astype(F32) * slot_w).astype(BF)
    split = width // 2
    near, far = core * split, (1 - core) * split
    cut = lambda array, at: lax.dynamic_slice_in_dim(array, at, split, 2)
    terms = (
        (arrived, dgate, "jrd,jrf->jdf"),
        (arrived, dup, "jrd,jrf->jdf"),
        (cots, weighted, "jrd,jrf->jfd"),
    )
    away = [ein32(spec, cut(left, far), right).astype(BF) for left, right, spec in terms]
    wide, away = lax.optimization_barrier((wide, away))
    away = [partner(array, "dp") for array in away]
    dweight = jnp.sum(jnp.sum(wide[:, :, units:].astype(F32), axis=2), axis=0)[:, None]
    wide = wide[:, :, :units]
    result = ein32("frk,fkc->rc", wide, down_cols).astype(BF)
    result = jnp.concatenate([result, halves(dweight, 128)], axis=1)
    result = jnp.transpose(result.reshape(per, n_ctx, quarter, -1), (1, 0, 2, 3))
    returned = swap(result.reshape(n_ctx, cap, -1), "ctx").reshape(n_ctx * cap, -1)
    grads = [
        (ein32(spec, cut(left, near), right) + other.astype(F32)).astype(BF)
        for (left, right, spec), other in zip(terms, away, strict=True)
    ]
    returned, grads = lax.optimization_barrier((returned, grads))
    dweight = jnp.sum(returned[:, wide_cols:].astype(F32), axis=1).reshape(n_ctx, cap, 1)
    returned = returned[:, :wide_cols]

    half = n_rows // 2
    combine = jnp.where(slots, route_b[:, None, :], jnp.zeros((), BF))
    combine = combine.reshape(n_ctx, held, cap, n_rows)
    combine = jnp.where(par == 0, combine[:, 0], combine[:, 1]).reshape(n_ctx * cap, n_rows)
    moe = lax.dot_general(
        combine, returned, (((0,), (0,)), ((), ())), preferred_element_type=F32
    )
    kept = lax.dynamic_slice_in_dim(moe, par * half, half, 0)
    sent = lax.dynamic_slice_in_dim(moe, (1 - par) * half, half, 0)
    own_hidden = lax.dynamic_slice(hidden, (par * half, col * wide_cols), (half, wide_cols))
    held_slots = slots.reshape(n_ctx, held, cap, n_rows)
    held_slots = jnp.where(par == 0, held_slots[:, 0], held_slots[:, 1])
    dweight = jnp.sum(jnp.where(held_slots, dweight, 0.0), axis=1)
    beside = jnp.pad(dweight, ((0, 0), (0, wide_cols - n_rows)))
    theirs = partner(jnp.concatenate([sent, beside], axis=0), "exp")
    out = own_hidden.astype(F32) + (kept + theirs[:half])
    theirs = theirs[half:, :n_rows]
    gathered_out = spread(out.astype(BF), "exp")
    out = gathered_out.reshape(n_exp // 2, 2, half, wide_cols)
    layer_out = jnp.transpose(out, (1, 2, 0, 3)).reshape(n_rows, width)

    dweight = jnp.stack(
        [jnp.where(par == 0, dweight, theirs), jnp.where(par == 0, theirs, dweight)], axis=1
    ).reshape(experts, n_rows)
    mean_term = jnp.sum(dweight * route_w, axis=0, keepdims=True)
    dprobs = jnp.where(hit, (dweight - mean_term) / chosen_sum, 0.0)
    dlogits = probs * (dprobs - jnp.sum(probs * dprobs, axis=0, keepdims=True))
    normed_cols = lax.dynamic_slice_in_dim(normed, me * (width // n_exp), width // n_exp, 1)
    term = jnp.dot(dlogits, normed_cols.astype(F32), precision=lax.Precision.HIGHEST)
    term = summed(term + partner(term, "dp"))
    term, _ = lax.optimization_barrier((term, gathered_out))
    router_grad = jnp.transpose(spread(term, "exp"), (0, 2, 1)).reshape(width, experts)
    return (layer_out[None], router_grad, *grads)


def solution(mesh):
    placed = (
        P("dp", "ctx", None),
        P("dp", "ctx", "exp", None),
        P("exp", None),
        P(),
        P("exp", None, None),
        P("exp", None),
        P(),
        P(),
        P("dp", "ctx", None),
        P("dp", "ctx"),
        P("ctx", None, "exp"),
        P("ctx", None, "exp"),
        P("ctx", "exp", None),
        P("dp", "ctx", None),
    )
    return jax.shard_map(
        local,
        mesh=mesh,
        in_specs=placed,
        out_specs=(
            P("dp", "ctx", None),
            P(),
            P("ctx", "dp", "exp"),
            P("ctx", "dp", "exp"),
            P("ctx", "exp", "dp"),
        ),
        check_vma=False,
    )
```

```python
import jax
import jax.numpy as jnp
import numpy as np
from jax import lax
from jax.experimental import pallas as pl
from jax.experimental.pallas import tpu as pltpu
from jax.sharding import PartitionSpec as P

ROPE = 64
NOPE = 128
DOCS = 4
epsilon = 1e-06
BF = jnp.bfloat16
F32 = jnp.float32


def swap(array, axis):
    return lax.all_to_all(array, axis, split_axis=0, concat_axis=0, tiled=True)


def spread(array, axis):
    count = lax.axis_size(axis)
    return swap(jnp.broadcast_to(array[None], (count, *array.shape)), axis)


def partner(array, axis):
    count = lax.axis_size(axis)
    return lax.ppermute(array, axis, [(i, i ^ 1) for i in range(count)])


def ringed(array, step):
    count = lax.axis_size("exp")
    return lax.ppermute(array, "exp", [(i, (i + step) % count) for i in range(count)])


def first_hop(array):
    return [array, ringed(array, 2), ringed(array, -2), partner(array, "exp")]


def second_hop(pieces):
    _, left, right, pair = pieces
    return [*pieces, ringed(left, 2), partner(left, "exp"), ringed(pair, -2)]


def third_hop(pieces):
    return [*pieces, partner(pieces[4], "exp")]


def gathered(array):
    return third_hop(second_hop(first_hop(array)))


def in_order(pieces):
    count = lax.axis_size("exp")
    me = lax.axis_index("exp")
    left, right, far = (me + count - 2) % count, (me + 2) % count, (me + 4) % count
    owners = jnp.stack([me, left, right, me ^ 1, far, left ^ 1, right ^ 1, far ^ 1])

    def body(owner, *refs):
        for n in range(count):
            refs[-1][owner[n]] = refs[n][...]

    whole = pl.BlockSpec(memory_space=pltpu.VMEM)
    return pl.pallas_call(
        body,
        out_shape=jax.ShapeDtypeStruct((count, *pieces[0].shape), pieces[0].dtype),
        in_specs=[pl.BlockSpec(memory_space=pltpu.SMEM)] + [whole] * count,
        out_specs=whole,
    )(owners, *pieces)


def summed(array):
    count = lax.axis_size("ctx")
    for stride, block in ((1, 4), (4, 16)):
        moved = [
            lax.ppermute(
                array,
                "ctx",
                [(i, i // block * block + (i + k * stride) % block) for i in range(count)],
            )
            for k in (1, 2, 3)
        ]
        array = (array + moved[1]) + (moved[0] + moved[2])
    return array


def halves(values, lanes):
    upper = lax.reduce_precision(values, exponent_bits=8, mantissa_bits=7)
    lane = jnp.arange(lanes, dtype=jnp.int32)
    return jnp.where(lane == 0, upper, jnp.where(lane == 1, values - upper, 0.0)).astype(BF)


def rms_scale(values, gain):
    return values * lax.rsqrt(jnp.mean(values * values, axis=-1, keepdims=True) + epsilon) * gain


def rotate(rope_part, positions):
    half_width = rope_part.shape[-1] // 2
    frequency = jnp.power(
        10000.0, -2.0 * jnp.arange(half_width, dtype=F32) / rope_part.shape[-1]
    )
    angles = positions.astype(F32)[:, None] * frequency[None, :]
    cosine = jnp.cos(angles)
    sine_part = jnp.sin(angles)
    first_half = rope_part[:, :half_width]
    second = rope_part[:, half_width:]
    return jnp.concatenate(
        [first_half * cosine - second * sine_part, second * cosine + first_half * sine_part], axis=1
    )


def dot32(a, b):
    return jnp.dot(a, b, preferred_element_type=F32)


def ein32(spec, a, b):
    return jnp.einsum(spec, a, b, preferred_element_type=F32)


def local(
    tokens,
    queries,
    kv_weight,
    kv_gain,
    uv_weight,
    out_weight,
    post_gain,
    router_weight,
    expert_ids,
    doc_ids,
    gate_weight,
    up_weight,
    down_weight,
    cotangent,
):
    rows = tokens[0]
    cot_rows = cotangent[0]
    ids = expert_ids[0]
    docs = doc_ids[0]
    n_rows, width = rows.shape
    latent_width = kv_gain.shape[0]
    n_exp = lax.axis_size("exp")
    n_ctx = lax.axis_size("ctx")
    me = lax.axis_index("exp")
    col, par = me // 2, me % 2
    block = lax.axis_index("ctx")
    core = lax.axis_index("dp")
    experts = router_weight.shape[1]
    held = experts // n_ctx
    cap = 32
    quarter = held * cap // n_exp
    per = cap // quarter
    heads = queries.shape[2]

    expert_of = jnp.arange(experts, dtype=jnp.int32)
    hit = jnp.any(ids.T[None, :, :] == expert_of[:, None, None], axis=1)
    before = jnp.asarray(np.triu(np.ones((n_rows, n_rows)), 1), BF)
    rank = dot32(hit.astype(BF), before).astype(jnp.int32)
    rank = jnp.where(hit, rank, -1)
    slots = rank[:, None, :] == jnp.arange(cap, dtype=jnp.int32)[None, :, None]
    mine = rank.reshape(n_ctx, held, n_rows)
    mine = jnp.where(me // per == 0, mine[:, 0], mine[:, 1])
    pick = mine[:, None, :] == (
        (me % per) * quarter + jnp.arange(quarter, dtype=jnp.int32)[None, :, None]
    )
    pick = pick.astype(BF).reshape(n_ctx * quarter, n_rows)

    def dispatch(values):
        out = dot32(pick, values).astype(BF).reshape(n_ctx, quarter, width)
        return swap(out, "ctx").reshape(n_ctx * quarter, width)

    def shared(out):
        return in_order(out).reshape(held, per * n_ctx * quarter, width)

    share = n_rows // n_exp
    kv_rows = kv_weight.shape[0]
    columns = lax.dynamic_slice_in_dim(rows, me * kv_rows, kv_rows, 1)
    part = dot32(columns, kv_weight).reshape(n_exp, share, -1)
    compressed = jnp.sum(swap(part, "exp"), axis=0)
    positions = block * n_rows + me * share + jnp.arange(share, dtype=jnp.int32)
    latent = rms_scale(compressed[:, :latent_width], kv_gain.astype(F32)).astype(BF)
    rope_key = rotate(compressed[:, latent_width:], positions).astype(BF)
    docs_share = lax.dynamic_slice_in_dim(docs, me * share, share, 0)
    doc_of = jnp.arange(64, dtype=jnp.int32)
    doc_key = (docs_share[:, None] == doc_of[None, :]).astype(BF)
    keys = jnp.concatenate([latent, rope_key, doc_key], axis=1)
    keys = spread(keys, "ctx").reshape(n_ctx * share, -1)
    cots = dispatch(cot_rows)
    pieces = gathered(keys)
    pieces, cots = lax.optimization_barrier((pieces, cots))
    cots = gathered(cots)
    wide_cols = 2 * width // n_exp
    units = gate_weight.shape[2]
    keys = jnp.concatenate(pieces, axis=0)
    left, right, far = (me + n_exp - 2) % n_exp, (me + 2) % n_exp, (me + 4) % n_exp
    owner = jnp.stack([me, left, right, me ^ 1, far, left ^ 1, right ^ 1, far ^ 1])
    in_block = np.arange(n_ctx * share, dtype=np.int32)
    in_block = in_block // share * n_rows + in_block % share
    key_at = (owner[:, None] * share + jnp.asarray(in_block)[None, :]).reshape(1, -1)

    differs = (doc_of[None, :] < DOCS) & (docs[:, None] != doc_of[None, :])
    doc_query = jnp.where(differs, -1e30, 0.0).astype(BF)
    query = jnp.concatenate(
        [
            jnp.transpose(queries[0], (1, 0, 2)),
            jnp.broadcast_to(doc_query[None], (heads, *doc_query.shape)),
        ],
        axis=2,
    ).reshape(heads * n_rows, -1)
    query_at = block * n_rows + jnp.arange(n_rows, dtype=jnp.int32)
    score_scale = (NOPE + ROPE) ** (-0.5)
    scores = ein32("qd,kd->qk", query, keys).reshape(heads, n_rows, -1)
    reached = (key_at <= query_at[:, None])[None]
    scores = jnp.where(reached, scores * score_scale, -1e30)
    weights = jnp.exp(scores - jnp.max(scores, axis=-1, keepdims=True))
    total = jnp.sum(weights, axis=-1, keepdims=True)
    mixed = (ein32("hqk,kl->hql", weights.astype(BF), keys[:, :latent_width]) / total).astype(BF)
    head_values = jnp.concatenate(
        [dot32(mixed[h], uv_weight[h]).astype(BF) for h in range(heads)], axis=1
    )
    part = dot32(head_values, out_weight).astype(BF).reshape(n_exp, share, width)
    attention = jnp.sum(swap(part, "exp").astype(F32), axis=0)
    own_rows = lax.dynamic_slice_in_dim(rows, me * share, share, 0).astype(F32)
    hidden = spread((own_rows + attention).astype(BF), "exp")
    hidden = hidden.reshape(n_rows, width)
    normed = rms_scale(hidden.astype(F32), post_gain.astype(F32)).astype(BF)
    arrived = dispatch(normed)

    logits = lax.dot_general(
        router_weight, normed, (((0,), (1,)), ((), ())), preferred_element_type=F32
    )
    probs = jax.nn.softmax(logits, axis=0)
    chosen = jnp.where(hit, probs, 0.0)
    chosen_sum = jnp.sum(chosen, axis=0, keepdims=True)
    route_w = chosen / chosen_sum
    route_b = route_w.astype(BF)
    slot_w = jnp.sum(jnp.where(slots, route_b.astype(F32)[:, None, :], 0.0), axis=2)
    slot_w = slot_w.reshape(n_ctx, held * cap)
    arrived = first_hop(arrived)
    down_cols = lax.dynamic_slice_in_dim(down_weight, core * (units // 2), units // 2, 1)
    down_cols = down_cols.reshape(held, units // 2, per, wide_cols)
    arrived, slot_w, cots = lax.optimization_barrier((arrived, slot_w, cots))
    arrived = second_hop(arrived)
    cots = shared(cots)
    dact = ein32("jrd,jfd->jrf", cots, down_weight)
    arrived, down_cols, dact = lax.optimization_barrier((arrived, down_cols, dact))
    arrived = third_hop(arrived)
    slot_w = swap(slot_w, "ctx")
    down_cols = jnp.transpose(down_cols, (2, 0, 1, 3)).reshape(n_exp, units // 2, wide_cols)
    down_cols = swap(down_cols, "exp")
    down_other = partner(down_cols, "dp")
    down_cols = jnp.concatenate(
        [
            jnp.where(core == 0, down_cols, down_other),
            jnp.where(core == 0, down_other, down_cols),
        ],
        axis=1,
    )
    slot_w = jnp.transpose(slot_w.reshape(n_ctx, held, per, quarter), (1, 2, 0, 3))
    slot_w = slot_w.reshape(held, -1, 1)
    arrived[7], slot_w = lax.optimization_barrier((arrived[7], slot_w))
    arrived = shared(arrived)

    gate_pre = ein32("jrd,jdf->jrf", arrived, gate_weight)
    up_pre = ein32("jrd,jdf->jrf", arrived, up_weight)
    sigmoid_gate = jax.nn.sigmoid(gate_pre)
    activated = (gate_pre * sigmoid_gate * up_pre).astype(BF)
    dweight = jnp.sum(activated.astype(F32) * dact, axis=2, keepdims=True)
    wide = jnp.concatenate([activated, halves(dweight, 16)], axis=2)
    wide = jnp.broadcast_to(wide[None], (n_exp // held, *wide.shape))
    wide = swap(wide.reshape(n_exp, *wide.shape[2:]), "exp")
    dact = dact * slot_w
    dgate = (dact * up_pre * sigmoid_gate * (1.0 + gate_pre * (1.0 - sigmoid_gate))).astype(BF)
    dup = (dact * gate_pre * sigmoid_gate).astype(BF)
    weighted = (activated.astype(F32) * slot_w).astype(BF)
    split = width // 2
    near, far = core * split, (1 - core) * split
    cut = lambda array, at: lax.dynamic_slice_in_dim(array, at, split, 2)
    terms = (
        (arrived, dgate, "jrd,jrf->jdf"),
        (arrived, dup, "jrd,jrf->jdf"),
        (cots, weighted, "jrd,jrf->jfd"),
    )
    away = [ein32(spec, cut(left, far), right).astype(BF) for left, right, spec in terms]
    wide, away = lax.optimization_barrier((wide, away))
    away = [partner(array, "dp") for array in away]
    dweight = jnp.sum(jnp.sum(wide[:, :, units:].astype(F32), axis=2), axis=0)[:, None]
    wide = wide[:, :, :units]
    result = ein32("frk,fkc->rc", wide, down_cols).astype(BF)
    result = jnp.concatenate([result, halves(dweight, 128)], axis=1)
    result = jnp.transpose(result.reshape(per, n_ctx, quarter, -1), (1, 0, 2, 3))
    returned = swap(result.reshape(n_ctx, cap, -1), "ctx").reshape(n_ctx * cap, -1)
    grads = [
        (ein32(spec, cut(left, near), right) + other.astype(F32)).astype(BF)
        for (left, right, spec), other in zip(terms, away, strict=True)
    ]
    returned, grads = lax.optimization_barrier((returned, grads))
    dweight = jnp.sum(returned[:, wide_cols:].astype(F32), axis=1).reshape(n_ctx, cap, 1)
    returned = returned[:, :wide_cols]

    half = n_rows // 2
    combine = jnp.where(slots, route_b[:, None, :], jnp.zeros((), BF))
    combine = combine.reshape(n_ctx, held, cap, n_rows)
    combine = jnp.where(par == 0, combine[:, 0], combine[:, 1]).reshape(n_ctx * cap, n_rows)
    moe = lax.dot_general(
        combine, returned, (((0,), (0,)), ((), ())), preferred_element_type=F32
    )
    kept = lax.dynamic_slice_in_dim(moe, par * half, half, 0)
    sent = lax.dynamic_slice_in_dim(moe, (1 - par) * half, half, 0)
    own_hidden = lax.dynamic_slice(hidden, (par * half, col * wide_cols), (half, wide_cols))
    held_slots = slots.reshape(n_ctx, held, cap, n_rows)
    held_slots = jnp.where(par == 0, held_slots[:, 0], held_slots[:, 1])
    dweight = jnp.sum(jnp.where(held_slots, dweight, 0.0), axis=1)
    beside = jnp.pad(dweight, ((0, 0), (0, wide_cols - n_rows)))
    theirs = partner(jnp.concatenate([sent, beside], axis=0), "exp")
    out = own_hidden.astype(F32) + (kept + theirs[:half])
    theirs = theirs[half:, :n_rows]
    gathered_out = spread(out.astype(BF), "exp")
    out = gathered_out.reshape(n_exp // 2, 2, half, wide_cols)
    layer_out = jnp.transpose(out, (1, 2, 0, 3)).reshape(n_rows, width)

    dweight = jnp.stack(
        [jnp.where(par == 0, dweight, theirs), jnp.where(par == 0, theirs, dweight)], axis=1
    ).reshape(experts, n_rows)
    mean_term = jnp.sum(dweight * route_w, axis=0, keepdims=True)
    dprobs = jnp.where(hit, (dweight - mean_term) / chosen_sum, 0.0)
    dlogits = probs * (dprobs - jnp.sum(probs * dprobs, axis=0, keepdims=True))
    normed_cols = lax.dynamic_slice_in_dim(normed, me * (width // n_exp), width // n_exp, 1)
    term = jnp.dot(dlogits, normed_cols.astype(F32), precision=lax.Precision.HIGHEST)
    term = summed(term + partner(term, "dp"))
    term, _ = lax.optimization_barrier((term, gathered_out))
    router_grad = jnp.transpose(spread(term, "exp"), (0, 2, 1)).reshape(width, experts)
    return (layer_out[None], router_grad, *grads)


def solution(mesh):
    placed = (
        P("dp", "ctx", None),
        P("dp", "ctx", "exp", None),
        P("exp", None),
        P(),
        P("exp", None, None),
        P("exp", None),
        P(),
        P(),
        P("dp", "ctx", None),
        P("dp", "ctx"),
        P("ctx", None, "exp"),
        P("ctx", None, "exp"),
        P("ctx", "exp", None),
        P("dp", "ctx", None),
    )
    return jax.shard_map(
        local,
        mesh=mesh,
        in_specs=placed,
        out_specs=(
            P("dp", "ctx", None),
            P(),
            P("ctx", "dp", "exp"),
            P("ctx", "dp", "exp"),
            P("ctx", "exp", "dp"),
        ),
        check_vma=False,
    )
```

```python
import jax
import jax.numpy as jnp
import numpy as np
from jax import lax
from jax.experimental import pallas as pl
from jax.experimental.pallas import tpu as pltpu
from jax.sharding import PartitionSpec as P

ROPE = 64
NOPE = 128
DOCS = 4
epsilon = 1e-06
BF = jnp.bfloat16
F32 = jnp.float32


def swap(array, axis):
    return lax.all_to_all(array, axis, split_axis=0, concat_axis=0, tiled=True)


def spread(array, axis):
    count = lax.axis_size(axis)
    return swap(jnp.broadcast_to(array[None], (count, *array.shape)), axis)


def partner(array, axis):
    count = lax.axis_size(axis)
    return lax.ppermute(array, axis, [(i, i ^ 1) for i in range(count)])


def ringed(array, step):
    count = lax.axis_size("exp")
    return lax.ppermute(array, "exp", [(i, (i + step) % count) for i in range(count)])


def first_hop(array):
    return [array, ringed(array, 2), ringed(array, -2), partner(array, "exp")]


def second_hop(pieces):
    _, left, right, pair = pieces
    return [*pieces, ringed(left, 2), partner(left, "exp"), ringed(pair, -2)]


def third_hop(pieces):
    return [*pieces, partner(pieces[4], "exp")]


def gathered(array):
    return third_hop(second_hop(first_hop(array)))


def in_order(pieces):
    count = lax.axis_size("exp")
    me = lax.axis_index("exp")
    left, right, far = (me + count - 2) % count, (me + 2) % count, (me + 4) % count
    owners = [me, left, right, me ^ 1, far, left ^ 1, right ^ 1, far ^ 1]
    out = jnp.zeros((count, *pieces[0].shape), pieces[0].dtype)
    for piece, owner in zip(pieces, owners, strict=True):
        out = lax.dynamic_update_slice(out, piece[None], (owner, 0, 0))
    return out


def put_in_order(pieces):
    count = lax.axis_size("exp")
    me = lax.axis_index("exp")
    left, right, far = (me + count - 2) % count, (me + 2) % count, (me + 4) % count
    owners = jnp.stack([me, left, right, me ^ 1, far, left ^ 1, right ^ 1, far ^ 1])

    def body(owner, *refs):
        for n in range(count):
            refs[-1][owner[n]] = refs[n][...]

    whole = pl.BlockSpec(memory_space=pltpu.VMEM)
    return pl.pallas_call(
        body,
        out_shape=jax.ShapeDtypeStruct((count, *pieces[0].shape), pieces[0].dtype),
        in_specs=[pl.BlockSpec(memory_space=pltpu.SMEM)] + [whole] * count,
        out_specs=whole,
    )(owners, *pieces)


def summed(array):
    count = lax.axis_size("ctx")
    for stride, block in ((1, 4), (4, 16)):
        moved = [
            lax.ppermute(
                array,
                "ctx",
                [(i, i // block * block + (i + k * stride) % block) for i in range(count)],
            )
            for k in (1, 2, 3)
        ]
        array = (array + moved[1]) + (moved[0] + moved[2])
    return array


def halves(values, lanes):
    upper = lax.reduce_precision(values, exponent_bits=8, mantissa_bits=7)
    lane = jnp.arange(lanes, dtype=jnp.int32)
    return jnp.where(lane == 0, upper, jnp.where(lane == 1, values - upper, 0.0)).astype(BF)


def rms_scale(values, gain):
    return values * lax.rsqrt(jnp.mean(values * values, axis=-1, keepdims=True) + epsilon) * gain


def rotate(rope_part, positions):
    half_width = rope_part.shape[-1] // 2
    frequency = jnp.power(
        10000.0, -2.0 * jnp.arange(half_width, dtype=F32) / rope_part.shape[-1]
    )
    angles = positions.astype(F32)[:, None] * frequency[None, :]
    cosine = jnp.cos(angles)
    sine_part = jnp.sin(angles)
    first_half = rope_part[:, :half_width]
    second = rope_part[:, half_width:]
    return jnp.concatenate(
        [first_half * cosine - second * sine_part, second * cosine + first_half * sine_part], axis=1
    )


def dot32(a, b):
    return jnp.dot(a, b, preferred_element_type=F32)


def ein32(spec, a, b):
    return jnp.einsum(spec, a, b, preferred_element_type=F32)


def local(
    tokens,
    queries,
    kv_weight,
    kv_gain,
    uv_weight,
    out_weight,
    post_gain,
    router_weight,
    expert_ids,
    doc_ids,
    gate_weight,
    up_weight,
    down_weight,
    cotangent,
):
    rows = tokens[0]
    cot_rows = cotangent[0]
    ids = expert_ids[0]
    docs = doc_ids[0]
    n_rows, width = rows.shape
    latent_width = kv_gain.shape[0]
    n_exp = lax.axis_size("exp")
    n_ctx = lax.axis_size("ctx")
    me = lax.axis_index("exp")
    col, par = me // 2, me % 2
    block = lax.axis_index("ctx")
    core = lax.axis_index("dp")
    experts = router_weight.shape[1]
    held = experts // n_ctx
    cap = 32
    quarter = held * cap // n_exp
    per = cap // quarter
    heads = queries.shape[2]

    expert_of = jnp.arange(experts, dtype=jnp.int32)
    hit = jnp.any(ids.T[None, :, :] == expert_of[:, None, None], axis=1)
    before = jnp.asarray(np.triu(np.ones((n_rows, n_rows)), 1), BF)
    rank = dot32(hit.astype(BF), before).astype(jnp.int32)
    rank = jnp.where(hit, rank, -1)
    slots = rank[:, None, :] == jnp.arange(cap, dtype=jnp.int32)[None, :, None]
    mine = rank.reshape(n_ctx, held, n_rows)
    mine = jnp.where(me // per == 0, mine[:, 0], mine[:, 1])
    pick = mine[:, None, :] == (
        (me % per) * quarter + jnp.arange(quarter, dtype=jnp.int32)[None, :, None]
    )
    pick = pick.astype(BF).reshape(n_ctx * quarter, n_rows)

    def dispatch(values):
        out = dot32(pick, values).astype(BF).reshape(n_ctx, quarter, width)
        return swap(out, "ctx").reshape(n_ctx * quarter, width)

    def shared(out):
        return in_order(out).reshape(held, per * n_ctx * quarter, width)

    share = n_rows // n_exp
    kv_rows = kv_weight.shape[0]
    columns = lax.dynamic_slice_in_dim(rows, me * kv_rows, kv_rows, 1)
    part = dot32(columns, kv_weight).reshape(n_exp, share, -1)
    compressed = jnp.sum(swap(part, "exp"), axis=0)
    positions = block * n_rows + me * share + jnp.arange(share, dtype=jnp.int32)
    latent = rms_scale(compressed[:, :latent_width], kv_gain.astype(F32)).astype(BF)
    rope_key = rotate(compressed[:, latent_width:], positions).astype(BF)
    docs_share = lax.dynamic_slice_in_dim(docs, me * share, share, 0)
    doc_of = jnp.arange(64, dtype=jnp.int32)
    doc_key = (docs_share[:, None] == doc_of[None, :]).astype(BF)
    keys = jnp.concatenate([latent, rope_key, doc_key], axis=1)
    keys = spread(keys, "ctx").reshape(n_ctx * share, -1)
    cots = dispatch(cot_rows)
    pieces = gathered(keys)
    pieces, cots = lax.optimization_barrier((pieces, cots))
    cots = shared(gathered(cots))
    wide_cols = 2 * width // n_exp
    units = gate_weight.shape[2]
    keys = jnp.concatenate(pieces, axis=0)
    left, right, far = (me + n_exp - 2) % n_exp, (me + 2) % n_exp, (me + 4) % n_exp
    owner = jnp.stack([me, left, right, me ^ 1, far, left ^ 1, right ^ 1, far ^ 1])
    in_block = np.arange(n_ctx * share, dtype=np.int32)
    in_block = in_block // share * n_rows + in_block % share
    key_at = (owner[:, None] * share + jnp.asarray(in_block)[None, :]).reshape(1, -1)

    differs = (doc_of[None, :] < DOCS) & (docs[:, None] != doc_of[None, :])
    doc_query = jnp.where(differs, -1e30, 0.0).astype(BF)
    query = jnp.concatenate(
        [
            jnp.transpose(queries[0], (1, 0, 2)),
            jnp.broadcast_to(doc_query[None], (heads, *doc_query.shape)),
        ],
        axis=2,
    ).reshape(heads * n_rows, -1)
    query_at = block * n_rows + jnp.arange(n_rows, dtype=jnp.int32)
    score_scale = (NOPE + ROPE) ** (-0.5)
    scores = ein32("qd,kd->qk", query, keys).reshape(heads, n_rows, -1)
    reached = (key_at <= query_at[:, None])[None]
    scores = jnp.where(reached, scores * score_scale, -1e30)
    weights = jnp.exp(scores - jnp.max(scores, axis=-1, keepdims=True))
    total = jnp.sum(weights, axis=-1, keepdims=True)
    mixed = (ein32("hqk,kl->hql", weights.astype(BF), keys[:, :latent_width]) / total).astype(BF)
    head_values = jnp.concatenate(
        [dot32(mixed[h], uv_weight[h]).astype(BF) for h in range(heads)], axis=1
    )
    part = dot32(head_values, out_weight).astype(BF).reshape(n_exp, share, width)
    attention = jnp.sum(swap(part, "exp").astype(F32), axis=0)
    own_rows = lax.dynamic_slice_in_dim(rows, me * share, share, 0).astype(F32)
    hidden = spread((own_rows + attention).astype(BF), "exp")
    hidden = hidden.reshape(n_rows, width)
    normed = rms_scale(hidden.astype(F32), post_gain.astype(F32)).astype(BF)
    arrived = dispatch(normed)

    logits = lax.dot_general(
        router_weight, normed, (((0,), (1,)), ((), ())), preferred_element_type=F32
    )
    probs = jax.nn.softmax(logits, axis=0)
    chosen = jnp.where(hit, probs, 0.0)
    chosen_sum = jnp.sum(chosen, axis=0, keepdims=True)
    route_w = chosen / chosen_sum
    route_b = route_w.astype(BF)
    slot_w = jnp.sum(jnp.where(slots, route_b.astype(F32)[:, None, :], 0.0), axis=2)
    slot_w = slot_w.reshape(n_ctx, held * cap)
    arrived = first_hop(arrived)
    down_cols = lax.dynamic_slice_in_dim(down_weight, core * (units // 2), units // 2, 1)
    down_cols = down_cols.reshape(held, units // 2, per, wide_cols)
    arrived, slot_w = lax.optimization_barrier((arrived, slot_w))
    arrived = second_hop(arrived)
    arrived = third_hop(arrived)
    dact = ein32("jrd,jfd->jrf", cots, down_weight)
    arrived, slot_w, dact, down_cols = lax.optimization_barrier(
        (arrived, swap(slot_w, "ctx"), dact, down_cols)
    )
    down_cols = jnp.transpose(down_cols, (2, 0, 1, 3)).reshape(n_exp, units // 2, wide_cols)
    down_cols = swap(down_cols, "exp")
    down_other = partner(down_cols, "dp")
    down_cols = jnp.concatenate(
        [
            jnp.where(core == 0, down_cols, down_other),
            jnp.where(core == 0, down_other, down_cols),
        ],
        axis=1,
    )
    slot_w = jnp.transpose(slot_w.reshape(n_ctx, held, per, quarter), (1, 2, 0, 3))
    slot_w = slot_w.reshape(held, -1, 1)
    arrived = put_in_order(arrived).reshape(held, per * n_ctx * quarter, width)

    gate_pre = ein32("jrd,jdf->jrf", arrived, gate_weight)
    up_pre = ein32("jrd,jdf->jrf", arrived, up_weight)
    sigmoid_gate = jax.nn.sigmoid(gate_pre)
    activated = (gate_pre * sigmoid_gate * up_pre).astype(BF)
    dweight = jnp.sum(activated.astype(F32) * dact, axis=2, keepdims=True)
    wide = jnp.concatenate([activated, halves(dweight, 16)], axis=2)
    wide = jnp.broadcast_to(wide[None], (n_exp // held, *wide.shape))
    wide = swap(wide.reshape(n_exp, *wide.shape[2:]), "exp")
    dact = dact * slot_w
    dgate = (dact * up_pre * sigmoid_gate * (1.0 + gate_pre * (1.0 - sigmoid_gate))).astype(BF)
    dup = (dact * gate_pre * sigmoid_gate).astype(BF)
    weighted = (activated.astype(F32) * slot_w).astype(BF)
    split = width // 2
    near, far = core * split, (1 - core) * split
    cut = lambda array, at: lax.dynamic_slice_in_dim(array, at, split, 2)
    terms = (
        (arrived, dgate, "jrd,jrf->jdf"),
        (arrived, dup, "jrd,jrf->jdf"),
        (cots, weighted, "jrd,jrf->jfd"),
    )
    away = [ein32(spec, cut(left, far), right).astype(BF) for left, right, spec in terms]
    wide, away = lax.optimization_barrier((wide, away))
    away = [partner(array, "dp") for array in away]
    dweight = jnp.sum(jnp.sum(wide[:, :, units:].astype(F32), axis=2), axis=0)[:, None]
    wide = wide[:, :, :units]
    result = ein32("frk,fkc->rc", wide, down_cols).astype(BF)
    result = jnp.concatenate([result, halves(dweight, 128)], axis=1)
    result = jnp.transpose(result.reshape(per, n_ctx, quarter, -1), (1, 0, 2, 3))
    returned = swap(result.reshape(n_ctx, cap, -1), "ctx").reshape(n_ctx * cap, -1)
    grads = [
        (ein32(spec, cut(left, near), right) + other.astype(F32)).astype(BF)
        for (left, right, spec), other in zip(terms, away, strict=True)
    ]
    returned, grads = lax.optimization_barrier((returned, grads))
    dweight = jnp.sum(returned[:, wide_cols:].astype(F32), axis=1).reshape(n_ctx, cap, 1)
    returned = returned[:, :wide_cols]

    half = n_rows // 2
    combine = jnp.where(slots, route_b[:, None, :], jnp.zeros((), BF))
    combine = combine.reshape(n_ctx, held, cap, n_rows)
    combine = jnp.where(par == 0, combine[:, 0], combine[:, 1]).reshape(n_ctx * cap, n_rows)
    moe = lax.dot_general(
        combine, returned, (((0,), (0,)), ((), ())), preferred_element_type=F32
    )
    kept = lax.dynamic_slice_in_dim(moe, par * half, half, 0)
    sent = lax.dynamic_slice_in_dim(moe, (1 - par) * half, half, 0)
    own_hidden = lax.dynamic_slice(hidden, (par * half, col * wide_cols), (half, wide_cols))
    held_slots = slots.reshape(n_ctx, held, cap, n_rows)
    held_slots = jnp.where(par == 0, held_slots[:, 0], held_slots[:, 1])
    dweight = jnp.sum(jnp.where(held_slots, dweight, 0.0), axis=1)
    beside = jnp.pad(dweight, ((0, 0), (0, wide_cols - n_rows)))
    theirs = partner(jnp.concatenate([sent, beside], axis=0), "exp")
    out = own_hidden.astype(F32) + (kept + theirs[:half])
    theirs = theirs[half:, :n_rows]
    gathered_out = spread(out.astype(BF), "exp")
    out = gathered_out.reshape(n_exp // 2, 2, half, wide_cols)
    layer_out = jnp.transpose(out, (1, 2, 0, 3)).reshape(n_rows, width)

    dweight = jnp.stack(
        [jnp.where(par == 0, dweight, theirs), jnp.where(par == 0, theirs, dweight)], axis=1
    ).reshape(experts, n_rows)
    mean_term = jnp.sum(dweight * route_w, axis=0, keepdims=True)
    dprobs = jnp.where(hit, (dweight - mean_term) / chosen_sum, 0.0)
    dlogits = probs * (dprobs - jnp.sum(probs * dprobs, axis=0, keepdims=True))
    normed_cols = lax.dynamic_slice_in_dim(normed, me * (width // n_exp), width // n_exp, 1)
    term = jnp.dot(dlogits, normed_cols.astype(F32), precision=lax.Precision.HIGHEST)
    term = summed(term + partner(term, "dp"))
    term, _ = lax.optimization_barrier((term, gathered_out))
    router_grad = jnp.transpose(spread(term, "exp"), (0, 2, 1)).reshape(width, experts)
    return (layer_out[None], router_grad, *grads)


def solution(mesh):
    placed = (
        P("dp", "ctx", None),
        P("dp", "ctx", "exp", None),
        P("exp", None),
        P(),
        P("exp", None, None),
        P("exp", None),
        P(),
        P(),
        P("dp", "ctx", None),
        P("dp", "ctx"),
        P("ctx", None, "exp"),
        P("ctx", None, "exp"),
        P("ctx", "exp", None),
        P("dp", "ctx", None),
    )
    return jax.shard_map(
        local,
        mesh=mesh,
        in_specs=placed,
        out_specs=(
            P("dp", "ctx", None),
            P(),
            P("ctx", "dp", "exp"),
            P("ctx", "dp", "exp"),
            P("ctx", "exp", "dp"),
        ),
        check_vma=False,
    )
```
